128 devices in a mesh: pts: 4 (over x_lo, core), comp: 32 (over x_hi, y, z).
Axes of the slice: x: 4 (x_hi: 2, x_lo: 2; x = x_hi * 2 + x_lo), y: 4, z: 4, core: 2. Of those that a mesh axis runs over, the one named last changes fastest.
Arguments:
- points: bfloat16 [1536, 512], P(('pts', 'comp')), may hold values from -28 to 28
- centres: bfloat16 [2048, 512], P('comp'), may hold values from -5 to 5
- whitening: bfloat16 [2048, 512, 512], P('comp', 'pts'), as said below
- log_prior: float32 [2048], P('comp'), may hold values from -4 to 4
Outputs:
- counts: float32 [2048], P('comp')
- first_moments: float32 [2048, 512], P('comp')
- second_moments: float32 [2048, 512, 512], P('comp', 'pts')
The draws below stay inside these ranges and needn't reach their ends.
Inputs may be any that keep to these rules, and one draw needn't show every extreme that they name: Each whitening[k] is lower triangular with diagonal entries between 0.69 and 2.82.
All inputs are finite; a program needn't handle non-finite values.
Results may differ from the reference program's by a relative error of at most 0.0029.
Values may be sent and summed in bfloat16 or wider, within the bound.
No kernel may reach another device: no remote copies, remote signals or barrier semaphores. Data moves between devices by JAX's collectives and lax.ppermute only.
A program may use at most 128 MiB of HBM per device.

```python
import math
import jax
import jax.numpy as jnp
from jax import lax

D = 512
K = 2048
NPTS = 1536


def draw_whitening(key, part):
    key_list = jax.random.split(key, K)
    row_index = lax.broadcasted_iota(jnp.int32, (D, D), 0)
    col_index = lax.broadcasted_iota(jnp.int32, (D, D), 1)
    lower = (row_index > col_index).astype(jnp.float32)
    ident = (row_index == col_index).astype(jnp.float32)

    def single(sub_key):
        key_scale, key_diag, key_off = jax.random.split(sub_key, 3)
        scale = jnp.exp(jax.random.uniform(key_scale, (), jnp.float32, math.log(0.7), math.log(1.4)))
        diag_vals = jnp.exp(jax.random.uniform(key_diag, (D,), jnp.float32, 0.0, math.log(2.0)))
        off_vals = jax.random.normal(key_off, (D, D), jnp.float32) * (0.6 / math.sqrt(D))
        return (scale * (off_vals * lower + ident * diag_vals[:, None])).astype(jnp.bfloat16)
    return lax.map(single, key_list)


def draw_points(key, part):
    key_base = jax.random.fold_in(key, 0)
    base = jnp.clip(jax.random.normal(key_base, (NPTS, D), jnp.float32), -4.0, 4.0)
    return base.astype(jnp.bfloat16)


def steps_of(stream_key, extent, cuts, least, largest):
    factor_of, own = 1.0, jax.random.fold_in(stream_key, 6)
    for position, parts in cuts:
        steps = jnp.exp(jax.random.uniform(jax.random.fold_in(own, position), (parts,), jnp.float32, least / len(cuts), largest / len(cuts)))
        factor_of = factor_of * jnp.repeat(steps, extent[position] // parts).reshape([-1 if axis == position else 1 for axis in range(len(extent))])
    return factor_of


def centred(own_key, shape, deviation, bound, shards=(), dtype=jnp.bfloat16):
    gain = steps_of(own_key, shape, shards, -0.22, 0.18) if shards else 1.0
    entries = jax.random.normal(own_key, shape, jnp.float32) * deviation * gain
    return jnp.minimum(jnp.maximum(entries, -bound), bound).astype(dtype)


def setup_inputs(seed: int = 0) -> dict:
    key_of = jax.random.split(jax.random.key(seed), 5)
    return {
        "points": draw_points(jax.random.fold_in(key_of[4], 71), 0),
        "centres": centred(key_of[1], (K, D), 1.0, 5.0, ((0, 32),)),
        "whitening": draw_whitening(jax.random.fold_in(key_of[4], 71), 0),
        "log_prior": centred(key_of[3], (K,), 1.0, 4.0, ((0, 32),), jnp.float32),
    }


anneal_beta = 1.25


def reference(points, centres, whitening, log_prior):
    points_f = points.astype(jnp.float32)
    blocks = K // 8
    factor_blocks = whitening.reshape(blocks, 8, D, D)
    centre_blocks = centres.reshape(blocks, 8, D)

    def block_dist(pair):
        factor, centre = pair
        factor_f = factor.astype(jnp.float32)
        offset = jnp.einsum("kqd,kd->kq", factor_f, centre.astype(jnp.float32))
        whitened = jnp.einsum("kqd,nd->kqn", factor_f, points_f) - offset[:, :, None]
        distance = jnp.sum(whitened * whitened, axis=1)
        logdet = jnp.sum(jnp.log(jnp.diagonal(factor_f, axis1=1, axis2=2)), axis=1)
        return distance, logdet

    distance, logdet = lax.map(block_dist, (factor_blocks, centre_blocks))
    distance = distance.reshape(K, NPTS)
    logdet = logdet.reshape(K)
    logits = anneal_beta * (log_prior[:, None] + (logdet[:, None] - 0.5 * distance) / D)
    row_peak = jnp.max(logits, axis=0)
    expo_vals = jnp.exp(logits - row_peak[None, :])
    responsibility = (expo_vals / jnp.sum(expo_vals, axis=0)[None, :]).astype(jnp.bfloat16)
    resp_f = responsibility.astype(jnp.float32)
    counts = jnp.sum(resp_f, axis=1)
    first_moments = jnp.dot(resp_f, points_f)
    points_t = points_f.T

    def block_second(resp_block):
        weighted = (resp_block[:, None, :] * points_t[None, :, :]).astype(jnp.bfloat16)
        weighted = lax.optimization_barrier(weighted).astype(jnp.float32)
        return jnp.einsum("kqn,nd->kqd", weighted, points_f)

    second_moments = lax.map(block_second, resp_f.reshape(blocks, 8, NPTS)).reshape(K, D, D)
    return counts, first_moments, second_moments
```

```python
import functools

import jax
import jax.numpy as jnp
from jax import lax
from jax.experimental import pallas as pl
from jax.experimental.pallas import tpu as pltpu
from jax.sharding import Mesh, PartitionSpec as P

D = 512
HALF = D // 2
BETA = 1.25
NT = (((1,), (1,)), ((), ()))
VMEM = 60 << 20
f32 = jnp.float32
bf16 = jnp.bfloat16
ALL = ("xl", "c", "xh", "y", "z")
CHIPS = ("xl", "xh", "y", "z")
COMP = ("xh", "y", "z")


def prep_kernel(pos, w_ref, wd_ref, c_ref, off_ref, ld_ref, *, kb):
    q = w_ref.shape[1]
    row = lax.broadcasted_iota(jnp.int32, (q, q), 0)
    eye = row == lax.broadcasted_iota(jnp.int32, (q, q), 1)
    for k in range(kb):
        prod = w_ref[k].astype(f32) * c_ref[k : k + 1, :].astype(f32)
        off_ref[0, :, k : k + 1] = jnp.sum(prod, axis=1, keepdims=True)
        diag = jnp.sum(jnp.where(eye, wd_ref[k].astype(f32), 0.0), axis=0, keepdims=True)
        total = jnp.sum(jnp.log(diag), axis=1, keepdims=True)
        ld_ref[k : k + 1, :] = jnp.broadcast_to(total, (1, 128))


def prep(pos, w, cen, kb=8):
    k, q, _ = w.shape
    spec = pltpu.PrefetchScalarGridSpec(
        num_scalar_prefetch=1,
        grid=(k // kb,),
        in_specs=[
            pl.BlockSpec((kb, q, D), lambda i, p: (i, 0, 0)),
            pl.BlockSpec((kb, q, q), lambda i, p: (i, 0, p[2])),
            pl.BlockSpec((kb, D), lambda i, p: (i, 0)),
        ],
        out_specs=[
            pl.BlockSpec((1, q, kb), lambda i, p: (i, 0, 0)),
            pl.BlockSpec((kb, 128), lambda i, p: (i, 0)),
        ],
    )
    return pl.pallas_call(
        functools.partial(prep_kernel, kb=kb),
        grid_spec=spec,
        out_shape=[
            jax.ShapeDtypeStruct((k // kb, q, kb), f32),
            jax.ShapeDtypeStruct((k, 128), f32),
        ],
        cost_estimate=pl.CostEstimate(flops=8_000_000, bytes_accessed=10_500_000, transcendentals=8192),
        name="prep",
    )(pos, w, w, cen)


def dist_kernel(pos, w_ref, off_ref, ld_ref, xa_ref, xb_ref, o_ref, *, kb, nt, mine):
    q = w_ref.shape[1]
    n = o_ref.shape[1]
    c = pos[0]
    side = c if mine else 1 - c
    ca = pl.multiple_of(c * HALF, HALF)
    cb = pl.multiple_of((1 - c) * HALF, HALF)
    wa = w_ref[:, :, pl.ds(ca, HALF)].reshape(kb * q, HALF)
    wb = w_ref[:, :, pl.ds(cb, HALF)].reshape(kb * q, HALF)
    for t in range(n // nt):
        rows = pl.ds(pl.multiple_of(side * n + t * nt, nt), nt)
        y = lax.dot_general(wa, xa_ref[rows, :], NT, preferred_element_type=f32)
        y = y + lax.dot_general(wb, xb_ref[rows, :], NT, preferred_element_type=f32)
        for k in range(kb):
            u = y[k * q : (k + 1) * q] - off_ref[0, :, k : k + 1]
            part = 0.5 * jnp.sum(u * u, axis=0, keepdims=True) - ld_ref[k : k + 1, :1]
            o_ref[k : k + 1, t * nt : (t + 1) * nt] = part


def dist(pos, w, off, ld, xa, xb, mine, kb=8, nt=256):
    k, q, _ = w.shape
    n = xa.shape[0] // 2
    spec = pltpu.PrefetchScalarGridSpec(
        num_scalar_prefetch=1,
        grid=(k // kb,),
        in_specs=[
            pl.BlockSpec((kb, q, D), lambda i, p: (i, 0, 0)),
            pl.BlockSpec((1, q, kb), lambda i, p: (i, 0, 0)),
            pl.BlockSpec((kb, 128), lambda i, p: (i, 0)),
            pl.BlockSpec((2 * n, HALF), lambda i, p: (0, 0)),
            pl.BlockSpec((2 * n, HALF), lambda i, p: (0, 0)),
        ],
        out_specs=pl.BlockSpec((kb, n), lambda i, p: (i, 0)),
    )
    return pl.pallas_call(
        functools.partial(dist_kernel, kb=kb, nt=nt, mine=mine),
        grid_spec=spec,
        out_shape=jax.ShapeDtypeStruct((k, n), f32),
        compiler_params=pltpu.CompilerParams(vmem_limit_bytes=VMEM),
        cost_estimate=pl.CostEstimate(
            flops=2 * k * q * D * n, bytes_accessed=2 * k * q * D + 4 * n * D + 4 * k * n, transcendentals=0
        ),
        name="dist_keep" if mine else "dist_send",
    )(pos, w, off, ld, xa, xb)


def band_kernel(pos, xa_ref, xb_ref, o_ref):
    c, xl = pos[0], pos[1]
    cols = pl.ds(pl.multiple_of(c * 128, 128), 128)

    @pl.when(c == xl)
    def _():
        o_ref[...] = xa_ref[:, cols].astype(f32).T.astype(bf16)

    @pl.when(c != xl)
    def _():
        o_ref[...] = xb_ref[:, cols].astype(f32).T.astype(bf16)


def band(pos, xa, xb):
    n = xa.shape[0]
    spec = pltpu.PrefetchScalarGridSpec(
        num_scalar_prefetch=1,
        grid=(1,),
        in_specs=[pl.BlockSpec((n, HALF), lambda i, p: (0, 0))] * 2,
        out_specs=pl.BlockSpec((128, n), lambda i, p: (0, 0)),
    )
    return pl.pallas_call(
        band_kernel,
        grid_spec=spec,
        out_shape=jax.ShapeDtypeStruct((128, n), bf16),
        cost_estimate=pl.CostEstimate(flops=0, bytes_accessed=2_000_000, transcendentals=0),
        name="band",
    )(pos, xa, xb)


def sec_kernel(pos, ra_ref, rb_ref, xt_ref, xa_ref, xb_ref, o_ref, fm_ref, ct_ref, wt_ref, *, kb):
    q = xt_ref.shape[0]
    h = ra_ref.shape[1]
    c = pos[0]
    for r_ref, side in ((ra_ref, c), (rb_ref, 1 - c)):
        cols = pl.ds(pl.multiple_of(side * h, 128), h)
        xv = xt_ref[:, cols]
        for k in range(kb):
            wt_ref[k * q : (k + 1) * q, cols] = xv * r_ref[k : k + 1, :]
        wt_ref[kb * q : kb * q + kb, cols] = r_ref[...]
    ra_sum = jnp.sum(ra_ref[...].astype(f32), axis=1, keepdims=True)
    ct_ref[...] = ra_sum + jnp.sum(rb_ref[...].astype(f32), axis=1, keepdims=True)
    wt = wt_ref[...]
    for x_ref, side in ((xa_ref, c), (xb_ref, 1 - c)):
        cols = pl.ds(pl.multiple_of(side * HALF, HALF), HALF)
        y = jnp.dot(wt, x_ref[...], preferred_element_type=f32)
        o_ref[:, :, cols] = y[: kb * q].reshape(kb, q, HALF)
        fm_ref[:, cols] = y[kb * q : kb * q + kb]


def sec(pos, ra, rb, xt, xa, xb, kb=16):
    k, h = ra.shape
    n = xa.shape[0]
    q = xt.shape[0]
    spec = pltpu.PrefetchScalarGridSpec(
        num_scalar_prefetch=1,
        grid=(k // kb,),
        in_specs=[
            pl.BlockSpec((kb, h), lambda i, p: (i, 0)),
            pl.BlockSpec((kb, h), lambda i, p: (i, 0)),
            pl.BlockSpec((q, n), lambda i, p: (0, 0)),
            pl.BlockSpec((n, HALF), lambda i, p: (0, 0)),
            pl.BlockSpec((n, HALF), lambda i, p: (0, 0)),
        ],
        out_specs=[
            pl.BlockSpec((kb, q, D), lambda i, p: (i, 0, 0)),
            pl.BlockSpec((kb, D), lambda i, p: (i, 0)),
            pl.BlockSpec((kb, 1), lambda i, p: (i, 0)),
        ],
        scratch_shapes=[pltpu.VMEM((kb * q + kb, n), bf16)],
    )
    return pl.pallas_call(
        functools.partial(sec_kernel, kb=kb),
        grid_spec=spec,
        out_shape=[
            jax.ShapeDtypeStruct((k, q, D), f32),
            jax.ShapeDtypeStruct((k, D), f32),
            jax.ShapeDtypeStruct((k, 1), f32),
        ],
        compiler_params=pltpu.CompilerParams(vmem_limit_bytes=VMEM),
        cost_estimate=pl.CostEstimate(
            flops=2 * k * q * D * n, bytes_accessed=4 * k * q * D + 4 * n * D, transcendentals=0
        ),
        name="sec",
    )(pos, ra, rb, xt, xa, xb)


def swap(x, axis):
    return lax.ppermute(x, axis, [(0, 1), (1, 0)])


def body(points, centres, whitening, log_prior):
    c, xl = lax.axis_index("c"), lax.axis_index("xl")
    pos = jnp.stack([c, xl, xl * 2 + c]).astype(jnp.int32)
    chips = lax.psum(1, CHIPS)
    groups = lax.psum(1, COMP)

    cols = lax.all_to_all(points, "c", 1, 0, tiled=True)
    m = cols.shape[0]
    xa = lax.all_to_all(jnp.broadcast_to(cols[None], (chips, m, HALF)), CHIPS, 0, 0, tiled=True)
    xa = xa.reshape(chips * m, HALF)
    xb = swap(xa, "c")

    off, ld = prep(pos, whitening, centres)
    send = dist(pos, whitening, off, ld, xa, xb, mine=False)
    got = swap(send, "c")
    keep = dist(pos, whitening, off, ld, xa, xb, mine=True)
    chip_part = keep + got
    total = chip_part + swap(chip_part, "xl")
    xt = band(pos, xa, xb)

    logits = BETA * (log_prior[:, None] - total / D)
    peak = jnp.max(logits, axis=0)
    lse = peak + jnp.log(jnp.sum(jnp.exp(logits - peak[None, :]), axis=0))
    h = lse.shape[0]
    lanes = lse.reshape(1, h // 128, 128)
    others = lax.all_to_all(jnp.broadcast_to(lanes, (groups, h // 128, 128)), COMP, 0, 0, tiled=True)
    top = jnp.max(others, axis=0)
    norm = (top + jnp.log(jnp.sum(jnp.exp(others - top[None]), axis=0))).reshape(h)
    ra = jnp.exp(logits - norm[None, :]).astype(bf16)
    rb = swap(ra, "c")
    second, first, counts = sec(pos, ra, rb, xt, xa, xb)
    return counts[:, 0], first, second


def solution(mesh):
    sizes = (2, 2, 2, 4, 4)
    fine = Mesh(mesh.devices.reshape(sizes), ALL)
    band_axes = ("xl", "c")
    in_specs = (P(ALL, None), P(COMP, None), P(COMP, band_axes, None), P(COMP))
    out_specs = (P(COMP), P(COMP, None), P(COMP, band_axes, None))
    return jax.shard_map(body, mesh=fine, in_specs=in_specs, out_specs=out_specs, check_vma=False)
```

```python
import functools

import jax
import jax.numpy as jnp
from jax import lax
from jax.experimental import pallas as pl
from jax.experimental.pallas import tpu as pltpu
from jax.sharding import Mesh, PartitionSpec as P

D = 512
HALF = D // 2
BETA = 1.25
NT = (((1,), (1,)), ((), ()))
VMEM = 24 << 20
STREAM = 24 << 20
KB_DIST = 16
f32 = jnp.float32
bf16 = jnp.bfloat16
ALL = ("xl", "c", "xh", "y", "z")
CHIPS = ("xl", "xh", "y", "z")
COMP = ("xh", "y", "z")


def prep_kernel(pos, w_ref, wd_ref, c_ref, off_ref, ld_ref, *, kb):
    q = w_ref.shape[1]
    row = lax.broadcasted_iota(jnp.int32, (q, q), 0)
    eye = row == lax.broadcasted_iota(jnp.int32, (q, q), 1)
    for k in range(kb):
        prod = w_ref[k].astype(f32) * c_ref[k : k + 1, :].astype(f32)
        off_ref[0, :, k : k + 1] = jnp.sum(prod, axis=1, keepdims=True)
        diag = jnp.sum(jnp.where(eye, wd_ref[k].astype(f32), 0.0), axis=0, keepdims=True)
        total = jnp.sum(jnp.log(diag), axis=1, keepdims=True)
        ld_ref[k : k + 1, :] = jnp.broadcast_to(total, (1, 128))


def prep(pos, w, cen, kb=8):
    k, q, _ = w.shape
    spec = pltpu.PrefetchScalarGridSpec(
        num_scalar_prefetch=1,
        grid=(k // kb,),
        in_specs=[
            pl.BlockSpec((kb, q, D), lambda i, p: (i, 0, 0)),
            pl.BlockSpec((kb, q, q), lambda i, p: (i, 0, p[2])),
            pl.BlockSpec((kb, D), lambda i, p: (i, 0)),
        ],
        out_specs=[
            pl.BlockSpec((1, q, kb), lambda i, p: (i, 0, 0)),
            pl.BlockSpec((kb, 128), lambda i, p: (i, 0)),
        ],
    )
    return pl.pallas_call(
        functools.partial(prep_kernel, kb=kb),
        grid_spec=spec,
        out_shape=[
            jax.ShapeDtypeStruct((k // kb, q, kb), f32),
            jax.ShapeDtypeStruct((k, 128), f32),
        ],
        compiler_params=pltpu.CompilerParams(vmem_limit_bytes=STREAM),
        cost_estimate=pl.CostEstimate(flops=8_000_000, bytes_accessed=10_500_000, transcendentals=8192),
        name="prep",
    )(pos, w, w, cen)


def dist_kernel(pos, wa_ref, wb_ref, off_ref, ld_ref, xa_ref, xb_ref, send_ref, keep_ref, *, kb, nt):
    q = wa_ref.shape[1]
    n = keep_ref.shape[1]
    c = pos[0]
    wa = wa_ref[...].reshape(kb * q, HALF)
    wb = wb_ref[...].reshape(kb * q, HALF)
    for o_ref, side in ((send_ref, 1 - c), (keep_ref, c)):
        for t in range(n // nt):
            rows = pl.ds(pl.multiple_of(side * n + t * nt, nt), nt)
            y = lax.dot_general(wa, xa_ref[rows, :], NT, preferred_element_type=f32)
            y = y + lax.dot_general(wb, xb_ref[rows, :], NT, preferred_element_type=f32)
            for k in range(kb):
                u = y[k * q : (k + 1) * q] - off_ref[k // 8, :, k % 8 : k % 8 + 1]
                part = 0.5 * jnp.sum(u * u, axis=0, keepdims=True) - ld_ref[k : k + 1, :1]
                o_ref[k : k + 1, t * nt : (t + 1) * nt] = part


def dist(pos, w, off, ld, xa, xb, kb=KB_DIST, nt=256):
    k, q, _ = w.shape
    n = xa.shape[0] // 2
    whole = pl.BlockSpec(memory_space=pltpu.VMEM)
    spec = pltpu.PrefetchScalarGridSpec(
        num_scalar_prefetch=1,
        grid=(k // kb,),
        in_specs=[
            pl.BlockSpec((kb, q, HALF), lambda i, p: (i, 0, p[0])),
            pl.BlockSpec((kb, q, HALF), lambda i, p: (i, 0, 1 - p[0])),
            pl.BlockSpec((kb // 8, q, 8), lambda i, p: (i, 0, 0)),
            pl.BlockSpec((kb, 128), lambda i, p: (i, 0)),
            whole,
            whole,
        ],
        out_specs=[pl.BlockSpec((kb, n), lambda i, p: (i, 0))] * 2,
    )
    return pl.pallas_call(
        functools.partial(dist_kernel, kb=kb, nt=nt),
        grid_spec=spec,
        out_shape=[jax.ShapeDtypeStruct((k, n), f32)] * 2,
        compiler_params=pltpu.CompilerParams(vmem_limit_bytes=STREAM),
        cost_estimate=pl.CostEstimate(
            flops=4 * k * q * D * n, bytes_accessed=2 * k * q * D + 4 * n * D + 8 * k * n, transcendentals=0
        ),
        name="dist",
    )(pos, w, w, off, ld, xa, xb)


def band_kernel(pos, xa_ref, xb_ref, o_ref):
    c, xl = pos[0], pos[1]
    h = o_ref.shape[1] // 2
    cols = pl.ds(pl.multiple_of(c * 128, 128), 128)
    for x_ref, here in ((xa_ref, c == xl), (xb_ref, c != xl)):

        @pl.when(here)
        def _():
            for t, side in enumerate((c, 1 - c)):
                rows = pl.ds(pl.multiple_of(side * h, h), h)
                o_ref[:, t * h : (t + 1) * h] = x_ref[rows, cols].astype(f32).T.astype(bf16)


def band(pos, xa, xb):
    n = xa.shape[0]
    whole = pl.BlockSpec(memory_space=pltpu.VMEM)
    spec = pltpu.PrefetchScalarGridSpec(num_scalar_prefetch=1, grid=(1,), in_specs=[whole] * 2, out_specs=whole)
    return pl.pallas_call(
        band_kernel,
        grid_spec=spec,
        out_shape=jax.ShapeDtypeStruct((128, n), bf16),
        compiler_params=pltpu.CompilerParams(vmem_limit_bytes=8 << 20),
        cost_estimate=pl.CostEstimate(flops=0, bytes_accessed=2_000_000, transcendentals=0),
        name="band",
    )(pos, xa, xb)


def sec_kernel(pos, ra_ref, rb_ref, xt_ref, xa_ref, xb_ref, o_ref, fm_ref, ct_ref, wt_ref, *, kb):
    q = xt_ref.shape[0]
    h = ra_ref.shape[1]
    c = pos[0]
    i, j = pl.program_id(0), pl.program_id(1)

    @pl.when((i == 0) & (j == 0))
    def _():
        ones = jnp.ones((8, h), bf16)
        total = lax.dot_general(ones, ra_ref[...], NT, preferred_element_type=f32)
        total = total + lax.dot_general(ones, rb_ref[...], NT, preferred_element_type=f32)
        ct_ref[...] = total[:1]

    @pl.when(j == 0)
    def _():
        block = pl.ds(pl.multiple_of(i * kb, kb), kb)
        for t, r_ref in enumerate((ra_ref, rb_ref)):
            cols = slice(t * h, (t + 1) * h)
            xv = xt_ref[:, cols]
            r = r_ref[block, :]
            for k in range(kb):
                wt_ref[k * q : (k + 1) * q, cols] = xv * r[k : k + 1, :]
            wt_ref[kb * q :, cols] = r

    for x_ref, at in ((xa_ref, 0), (xb_ref, 1)):

        @pl.when(j == at)
        def _():
            mine = pl.ds(pl.multiple_of(c * h, h), h)
            other = pl.ds(pl.multiple_of((1 - c) * h, h), h)
            rows = jnp.concatenate([x_ref[mine, :], x_ref[other, :]], axis=0)
            y = jnp.dot(wt_ref[...], rows, preferred_element_type=f32)
            o_ref[...] = y[: kb * q].reshape(kb, q, HALF)
            fm_ref[...] = y[kb * q :]


def sec(pos, ra, rb, xt, xa, xb, kb=16):
    k, _ = ra.shape
    n = xa.shape[0]
    q = xt.shape[0]
    whole = pl.BlockSpec(memory_space=pltpu.VMEM)
    spec = pltpu.PrefetchScalarGridSpec(
        num_scalar_prefetch=1,
        grid=(k // kb, 2),
        in_specs=[whole] * 5,
        out_specs=[
            pl.BlockSpec((kb, q, HALF), lambda i, j, p: (i, 0, p[0] + j * (1 - 2 * p[0]))),
            pl.BlockSpec((kb, HALF), lambda i, j, p: (i, p[0] + j * (1 - 2 * p[0]))),
            pl.BlockSpec((1, k), lambda i, j, p: (0, 0)),
        ],
        scratch_shapes=[pltpu.VMEM((kb * q + kb, n), bf16)],
    )
    return pl.pallas_call(
        functools.partial(sec_kernel, kb=kb),
        grid_spec=spec,
        out_shape=[
            jax.ShapeDtypeStruct((k, q, D), f32),
            jax.ShapeDtypeStruct((k, D), f32),
            jax.ShapeDtypeStruct((1, k), f32),
        ],
        compiler_params=pltpu.CompilerParams(vmem_limit_bytes=VMEM),
        cost_estimate=pl.CostEstimate(
            flops=2 * k * q * D * n, bytes_accessed=4 * k * q * D + 4 * n * D, transcendentals=0
        ),
        name="sec",
    )(pos, ra, rb, xt, xa, xb)


def swap(x, axis):
    return lax.ppermute(x, axis, [(0, 1), (1, 0)])


def layer(points, centres, whitening, log_prior):
    c, xl = lax.axis_index("c"), lax.axis_index("xl")
    pos = jnp.stack([c, xl, xl * 2 + c]).astype(jnp.int32)
    chips = lax.psum(1, CHIPS)
    groups = lax.psum(1, COMP)

    whitening = pltpu.with_memory_space_constraint(whitening, pltpu.HBM)
    rows = points.shape[0]
    own = lax.dynamic_slice(points, (0, c * HALF), (rows, HALF))
    away = swap(lax.dynamic_slice(points, (0, (1 - c) * HALF), (rows, HALF)), "c")
    pair = jnp.where(c == 0, jnp.concatenate([own, away]), jnp.concatenate([away, own]))
    pieces = jnp.broadcast_to(pair[None], (chips, 2 * rows, HALF))
    xa = lax.all_to_all(pieces, CHIPS, 0, 0, tiled=True)
    xa = xa.reshape(chips * 2 * rows, HALF)
    xb = swap(xa, "c")

    off, ld = prep(pos, whitening, centres)
    send, keep = dist(pos, whitening, off, ld, xa, xb)
    chip_part = keep + swap(send, "c")
    total = chip_part + swap(chip_part, "xl")
    xt = band(pos, xa, xb)

    logits = BETA * (log_prior[:, None] - total / D)
    peak = jnp.max(logits, axis=0)
    lse = peak + jnp.log(jnp.sum(jnp.exp(logits - peak[None, :]), axis=0))
    h = lse.shape[0]
    lanes = jnp.broadcast_to(lse.reshape(1, h // 128, 128), (groups, h // 128, 128))
    others = lax.all_to_all(lanes, COMP, 0, 0, tiled=True)
    top = jnp.max(others, axis=0)
    norm = (top + jnp.log(jnp.sum(jnp.exp(others - top[None]), axis=0))).reshape(h)
    ra = jnp.exp(logits - norm[None, :]).astype(bf16)
    rb = swap(ra, "c")
    second, first, counts = sec(pos, ra, rb, xt, xa, xb)
    return counts.reshape(-1), first, second


def solution(mesh):
    fine = Mesh(mesh.devices.reshape(2, 2, 2, 4, 4), ALL)
    band_axes = ("xl", "c")
    in_specs = (P(ALL, None), P(COMP, None), P(COMP, band_axes, None), P(COMP))
    out_specs = (P(COMP), P(COMP, None), P(COMP, band_axes, None))
    return jax.shard_map(layer, mesh=fine, in_specs=in_specs, out_specs=out_specs, check_vma=False)
```

```python
import functools

import jax
import jax.numpy as jnp
from jax import lax
from jax.experimental import pallas as pl
from jax.experimental.pallas import tpu as pltpu
from jax.sharding import Mesh, PartitionSpec as P

D = 512
HALF = D // 2
BETA = 1.25
NT = (((1,), (1,)), ((), ()))
VMEM = 24 << 20
KB_DIST = 16
f32 = jnp.float32
bf16 = jnp.bfloat16
ALL = ("xl", "c", "xh", "y", "z")
CHIPS = ("xl", "xh", "y", "z")
COMP = ("xh", "y", "z")


def prep_kernel(pos, w_ref, wd_ref, c_ref, off_ref, ld_ref, *, kb):
    q = w_ref.shape[1]
    row = lax.broadcasted_iota(jnp.int32, (q, q), 0)
    eye = row == lax.broadcasted_iota(jnp.int32, (q, q), 1)
    for k in range(kb):
        prod = w_ref[k].astype(f32) * c_ref[k : k + 1, :].astype(f32)
        off_ref[0, :, k : k + 1] = jnp.sum(prod, axis=1, keepdims=True)
        diag = jnp.sum(jnp.where(eye, wd_ref[k].astype(f32), 0.0), axis=0, keepdims=True)
        total = jnp.sum(jnp.log(diag), axis=1, keepdims=True)
        ld_ref[k : k + 1, :] = jnp.broadcast_to(total, (1, 128))


def prep(pos, w, cen, kb=8):
    k, q, _ = w.shape
    spec = pltpu.PrefetchScalarGridSpec(
        num_scalar_prefetch=1,
        grid=(k // kb,),
        in_specs=[
            pl.BlockSpec((kb, q, D), lambda i, p: (i, 0, 0)),
            pl.BlockSpec((kb, q, q), lambda i, p: (i, 0, p[0])),
            pl.BlockSpec((kb, D), lambda i, p: (i, 0)),
        ],
        out_specs=[
            pl.BlockSpec((1, q, kb), lambda i, p: (i, 0, 0)),
            pl.BlockSpec((kb, 128), lambda i, p: (i, 0)),
        ],
    )
    return pl.pallas_call(
        functools.partial(prep_kernel, kb=kb),
        grid_spec=spec,
        out_shape=[
            jax.ShapeDtypeStruct((k // kb, q, kb), f32),
            jax.ShapeDtypeStruct((k, 128), f32),
        ],
        compiler_params=pltpu.CompilerParams(vmem_limit_bytes=VMEM),
        cost_estimate=pl.CostEstimate(flops=8_000_000, bytes_accessed=10_500_000, transcendentals=8192),
        name="prep",
    )(pos, w, w, cen)


def dist_kernel(w_ref, off_ref, ld_ref, x_ref, o_ref, *, kb, nt):
    q = w_ref.shape[1]
    n = o_ref.shape[1]
    w = w_ref[...].reshape(kb * q, D)
    for t in range(n // nt):
        y = lax.dot_general(w, x_ref[t * nt : (t + 1) * nt, :], NT, preferred_element_type=f32)
        for k in range(kb):
            u = y[k * q : (k + 1) * q] - off_ref[k // 8, :, k % 8 : k % 8 + 1]
            part = 0.5 * jnp.sum(u * u, axis=0, keepdims=True) - ld_ref[k : k + 1, :1]
            o_ref[k : k + 1, t * nt : (t + 1) * nt] = part


def dist(w, off, ld, x, kb=KB_DIST, nt=256):
    k, q, _ = w.shape
    n = x.shape[0]
    return pl.pallas_call(
        functools.partial(dist_kernel, kb=kb, nt=nt),
        grid=(k // kb,),
        in_specs=[
            pl.BlockSpec((kb, q, D), lambda i: (i, 0, 0)),
            pl.BlockSpec((kb // 8, q, 8), lambda i: (i, 0, 0)),
            pl.BlockSpec((kb, 128), lambda i: (i, 0)),
            pl.BlockSpec(memory_space=pltpu.VMEM),
        ],
        out_specs=pl.BlockSpec((kb, n), lambda i: (i, 0)),
        out_shape=jax.ShapeDtypeStruct((k, n), f32),
        compiler_params=pltpu.CompilerParams(vmem_limit_bytes=VMEM),
        cost_estimate=pl.CostEstimate(
            flops=2 * k * q * D * n, bytes_accessed=2 * k * q * D + 2 * n * D + 4 * k * n, transcendentals=0
        ),
        name="dist",
    )(w, off, ld, x)


def band_kernel(pos, xa_ref, xb_ref, o_ref):
    h = xa_ref.shape[0]
    cols = pl.ds(pl.multiple_of(pos[0] * 128, 128), 128)
    for t, x_ref in enumerate((xa_ref, xb_ref)):
        o_ref[:, t * h : (t + 1) * h] = x_ref[:, cols].astype(f32).T.astype(bf16)


def band(pos, xa, xb):
    h = xa.shape[0]
    whole = pl.BlockSpec(memory_space=pltpu.VMEM)
    spec = pltpu.PrefetchScalarGridSpec(num_scalar_prefetch=1, grid=(1,), in_specs=[whole] * 2, out_specs=whole)
    return pl.pallas_call(
        band_kernel,
        grid_spec=spec,
        out_shape=jax.ShapeDtypeStruct((128, 2 * h), bf16),
        compiler_params=pltpu.CompilerParams(vmem_limit_bytes=8 << 20),
        cost_estimate=pl.CostEstimate(flops=0, bytes_accessed=2_000_000, transcendentals=0),
        name="band",
    )(pos, xa, xb)


def sec_kernel(ra_ref, rb_ref, xt_ref, xa_ref, xb_ref, o_ref, fm_ref, ct_ref, wt_ref, *, kb):
    q = xt_ref.shape[0]
    h = ra_ref.shape[1]
    i, j = pl.program_id(0), pl.program_id(1)

    @pl.when((i == 0) & (j == 0))
    def _():
        ones = jnp.ones((8, h), bf16)
        total = lax.dot_general(ones, ra_ref[...], NT, preferred_element_type=f32)
        total = total + lax.dot_general(ones, rb_ref[...], NT, preferred_element_type=f32)
        ct_ref[...] = total[:1]

    @pl.when(j == 0)
    def _():
        block = pl.ds(pl.multiple_of(i * kb, kb), kb)
        for t, r_ref in enumerate((ra_ref, rb_ref)):
            cols = slice(t * h, (t + 1) * h)
            xv = xt_ref[:, cols]
            r = r_ref[block, :]
            for k in range(kb):
                wt_ref[k * q : (k + 1) * q, cols] = xv * r[k : k + 1, :]
            wt_ref[kb * q :, cols] = r

    for half in range(2):

        @pl.when(j == half)
        def _():
            cols = slice(half * HALF, (half + 1) * HALF)
            rows = jnp.concatenate([xa_ref[:, cols], xb_ref[:, cols]], axis=0)
            y = jnp.dot(wt_ref[...], rows, preferred_element_type=f32)
            o_ref[...] = y[: kb * q].reshape(kb, q, HALF)
            fm_ref[...] = y[kb * q :]


def sec(ra, rb, xt, xa, xb, kb=16):
    k, _ = ra.shape
    q, n = xt.shape
    whole = pl.BlockSpec(memory_space=pltpu.VMEM)
    return pl.pallas_call(
        functools.partial(sec_kernel, kb=kb),
        grid=(k // kb, 2),
        in_specs=[whole] * 5,
        out_specs=[
            pl.BlockSpec((kb, q, HALF), lambda i, j: (i, 0, j)),
            pl.BlockSpec((kb, HALF), lambda i, j: (i, j)),
            pl.BlockSpec((1, k), lambda i, j: (0, 0)),
        ],
        out_shape=[
            jax.ShapeDtypeStruct((k, q, D), f32),
            jax.ShapeDtypeStruct((k, D), f32),
            jax.ShapeDtypeStruct((1, k), f32),
        ],
        scratch_shapes=[pltpu.VMEM((kb * q + kb, n), bf16)],
        compiler_params=pltpu.CompilerParams(vmem_limit_bytes=VMEM),
        cost_estimate=pl.CostEstimate(
            flops=2 * k * q * D * n, bytes_accessed=4 * k * q * D + 2 * n * D, transcendentals=0
        ),
        name="sec",
    )(ra, rb, xt, xa, xb)


def swap(x, axis):
    return lax.ppermute(x, axis, [(0, 1), (1, 0)])


def log_sum(values):
    peak = jnp.max(values, axis=0)
    return peak + jnp.log(jnp.sum(jnp.exp(values - peak[None]), axis=0))


def layer(points, centres, whitening, log_prior):
    pos = (lax.axis_index("xl") * 2 + lax.axis_index("c")).astype(jnp.int32).reshape(1)
    chips = lax.psum(1, CHIPS)
    groups = lax.psum(1, COMP)
    whitening = pltpu.with_memory_space_constraint(whitening, pltpu.HBM)

    m = points.size // 128
    pieces = jnp.broadcast_to(points.reshape(1, m, 128), (chips, m, 128))
    xa = lax.all_to_all(pieces, CHIPS, 0, 0, tiled=True)
    xa = xa.reshape(chips * points.shape[0], D)
    xb = swap(xa, "c")

    off, ld = prep(pos, whitening, centres)
    send = dist(whitening, off, ld, xa)
    got = swap(send, "c")
    keep = dist(whitening, off, ld, xb)
    chip_part = keep + got
    total_b = chip_part + swap(chip_part, "xl")
    total_a = swap(total_b, "c")
    xt = band(pos, xa, xb)

    logits_a = BETA * (log_prior[:, None] - total_a / D)
    logits_b = BETA * (log_prior[:, None] - total_b / D)
    h = logits_a.shape[1]
    lse = jnp.concatenate([log_sum(logits_a), log_sum(logits_b)])
    lanes = jnp.broadcast_to(lse.reshape(1, 1, 2 * h), (groups, 1, 2 * h))
    others = lax.all_to_all(lanes, COMP, 0, 0, tiled=True)
    norm = log_sum(others.reshape(groups, 2 * h))
    ra = jnp.exp(logits_a - norm[None, :h]).astype(bf16)
    rb = jnp.exp(logits_b - norm[None, h:]).astype(bf16)
    second, first, counts = sec(ra, rb, xt, xa, xb)
    return counts.reshape(-1), first, second


def solution(mesh):
    fine = Mesh(mesh.devices.reshape(2, 2, 2, 4, 4), ALL)
    band_axes = ("xl", "c")
    in_specs = (P(ALL, None), P(COMP, None), P(COMP, band_axes, None), P(COMP))
    out_specs = (P(COMP), P(COMP, None), P(COMP, band_axes, None))
    return jax.shard_map(layer, mesh=fine, in_specs=in_specs, out_specs=out_specs, check_vma=False)
```

```python
import functools

import jax
import jax.numpy as jnp
from jax import lax
from jax.experimental import pallas as pl
from jax.experimental.pallas import tpu as pltpu
from jax.sharding import Mesh, PartitionSpec as P

D = 512
HALF = D // 2
BETA = 1.25
NT = (((1,), (1,)), ((), ()))
VMEM = 24 << 20
KB_DIST = 16
f32 = jnp.float32
bf16 = jnp.bfloat16
ALL = ("xl", "c", "xh", "y", "z")
CHIPS = ("xl", "xh", "y", "z")
COMP = ("xh", "y", "z")


def prep_kernel(pos, w_ref, wd_ref, c_ref, off_ref, ld_ref, *, kb):
    q = w_ref.shape[1]
    row = lax.broadcasted_iota(jnp.int32, (q, q), 0)
    eye = row == lax.broadcasted_iota(jnp.int32, (q, q), 1)
    for k in range(kb):
        prod = w_ref[k].astype(f32) * c_ref[k : k + 1, :].astype(f32)
        off_ref[0, :, k : k + 1] = jnp.sum(prod, axis=1, keepdims=True)
        diag = jnp.sum(jnp.where(eye, wd_ref[k].astype(f32), 0.0), axis=0, keepdims=True)
        total = jnp.sum(jnp.log(diag), axis=1, keepdims=True)
        ld_ref[k : k + 1, :] = jnp.broadcast_to(total, (1, 128))


def prep(pos, w, cen, kb=8):
    k, q, _ = w.shape
    spec = pltpu.PrefetchScalarGridSpec(
        num_scalar_prefetch=1,
        grid=(k // kb,),
        in_specs=[
            pl.BlockSpec((kb, q, D), lambda i, p: (i, 0, 0)),
            pl.BlockSpec((kb, q, q), lambda i, p: (i, 0, p[0])),
            pl.BlockSpec((kb, D), lambda i, p: (i, 0)),
        ],
        out_specs=[
            pl.BlockSpec((1, q, kb), lambda i, p: (i, 0, 0)),
            pl.BlockSpec((kb, 128), lambda i, p: (i, 0)),
        ],
    )
    return pl.pallas_call(
        functools.partial(prep_kernel, kb=kb),
        grid_spec=spec,
        out_shape=[
            jax.ShapeDtypeStruct((k // kb, q, kb), f32),
            jax.ShapeDtypeStruct((k, 128), f32),
        ],
        compiler_params=pltpu.CompilerParams(vmem_limit_bytes=VMEM),
        cost_estimate=pl.CostEstimate(flops=8_000_000, bytes_accessed=10_500_000, transcendentals=8192),
        name="prep",
    )(pos, w, w, cen)


def dist_block(w_ref, off_ref, ld_ref, x_ref, o_ref, i, kb, nt, start):
    q = w_ref.shape[1]
    n = o_ref.shape[1]
    block = pl.ds(pl.multiple_of(i * kb, kb), kb)
    w = w_ref[block].reshape(kb * q, D)
    ld = ld_ref[block, :]
    for t in range(n // nt):
        rows = slice(start + t * nt, start + (t + 1) * nt)
        y = lax.dot_general(w, x_ref[rows, :], NT, preferred_element_type=f32)
        parts = []
        for k in range(kb):
            u = y[k * q : (k + 1) * q] - off_ref[i * (kb // 8) + k // 8, :, k % 8 : k % 8 + 1]
            parts.append(0.5 * jnp.sum(u * u, axis=0, keepdims=True) - ld[k : k + 1, :1])
        o_ref[block, t * nt : (t + 1) * nt] = jnp.concatenate(parts, axis=0)


def first_kernel(w_hbm, off_ref, ld_ref, x_ref, o_ref, w_ref, sem, *, kb, nt):
    count = w_ref.shape[0]

    def copy(i):
        block = pl.ds(i * 8, 8)
        return pltpu.make_async_copy(w_hbm.at[block], w_ref.at[block], sem.at[i])

    for i in range(count // 8):
        copy(i).start()

    @pl.loop(0, count // kb)
    def _(i):
        for j in range(kb // 8):
            copy(i * (kb // 8) + j).wait()
        dist_block(w_ref, off_ref, ld_ref, x_ref, o_ref, i, kb, nt, 0)


def dist_kernel(w_ref, off_ref, ld_ref, x_ref, o_ref, *, kb, nt, start):
    @pl.loop(0, w_ref.shape[0] // kb)
    def _(i):
        dist_block(w_ref, off_ref, ld_ref, x_ref, o_ref, i, kb, nt, start)


def dist(w, off, ld, x, start, n, first=False, kb=KB_DIST, nt=256):
    k, q, _ = w.shape
    whole = pl.BlockSpec(memory_space=pltpu.VMEM)
    if first:
        kernel = functools.partial(first_kernel, kb=kb, nt=nt)
    else:
        kernel = functools.partial(dist_kernel, kb=kb, nt=nt, start=start)
    out = jax.ShapeDtypeStruct((k, n), f32)
    return pl.pallas_call(
        kernel,
        in_specs=[pl.BlockSpec(memory_space=pl.ANY) if first else whole] + [whole] * 3,
        out_specs=[whole, whole] if first else whole,
        out_shape=[out, jax.ShapeDtypeStruct(w.shape, bf16)] if first else out,
        scratch_shapes=[pltpu.SemaphoreType.DMA((k // 8,))] if first else [],
        compiler_params=pltpu.CompilerParams(vmem_limit_bytes=VMEM),
        cost_estimate=pl.CostEstimate(
            flops=2 * k * q * D * n, bytes_accessed=2 * k * q * D + 2 * n * D + 4 * k * n, transcendentals=0
        ),
        name="dist_first" if first else "dist",
    )(w, off, ld, x)


def rows_kernel(g_ref, o_ref, wide_ref):
    count, m, _ = g_ref.shape
    wide_ref[...] = g_ref[...].astype(f32).reshape(count * m, 128)
    n = o_ref.shape[0]
    parts = D // 128
    for b in range(parts):
        o_ref[:, b * 128 : (b + 1) * 128] = wide_ref[pl.ds(b, n, stride=parts), :].astype(bf16)


def to_rows(g):
    count, m, _ = g.shape
    whole = pl.BlockSpec(memory_space=pltpu.VMEM)
    return pl.pallas_call(
        rows_kernel,
        in_specs=[whole],
        out_specs=whole,
        out_shape=jax.ShapeDtypeStruct((count * m * 128 // D, D), bf16),
        scratch_shapes=[pltpu.VMEM((count * m, 128), f32)],
        compiler_params=pltpu.CompilerParams(vmem_limit_bytes=8 << 20),
        cost_estimate=pl.CostEstimate(flops=0, bytes_accessed=2_000_000, transcendentals=0),
        name="rows",
    )(g)


def band_kernel(pos, xa_ref, xb_ref, o_ref):
    h = xa_ref.shape[0]
    cols = pl.ds(pl.multiple_of(pos[0] * 128, 128), 128)
    for t, x_ref in enumerate((xa_ref, xb_ref)):
        o_ref[:, t * h : (t + 1) * h] = x_ref[:, cols].astype(f32).T.astype(bf16)


def band(pos, xa, xb):
    h = xa.shape[0]
    whole = pl.BlockSpec(memory_space=pltpu.VMEM)
    spec = pltpu.PrefetchScalarGridSpec(num_scalar_prefetch=1, grid=(1,), in_specs=[whole] * 2, out_specs=whole)
    return pl.pallas_call(
        band_kernel,
        grid_spec=spec,
        out_shape=jax.ShapeDtypeStruct((128, 2 * h), bf16),
        compiler_params=pltpu.CompilerParams(vmem_limit_bytes=8 << 20),
        cost_estimate=pl.CostEstimate(flops=0, bytes_accessed=2_000_000, transcendentals=0),
        name="band",
    )(pos, xa, xb)


def sec_kernel(ra_ref, rb_ref, xt_ref, xa_ref, xb_ref, o_ref, fm_ref, ct_ref, wt_ref, *, kb):
    q = xt_ref.shape[0]
    h = ra_ref.shape[1]
    i, j = pl.program_id(0), pl.program_id(1)

    @pl.when((i == 0) & (j == 0))
    def _():
        ones = jnp.ones((8, h), bf16)
        total = lax.dot_general(ones, ra_ref[...], NT, preferred_element_type=f32)
        total = total + lax.dot_general(ones, rb_ref[...], NT, preferred_element_type=f32)
        ct_ref[...] = total[:1]

    @pl.when(j == 0)
    def _():
        block = pl.ds(pl.multiple_of(i * kb, kb), kb)
        for t, r_ref in enumerate((ra_ref, rb_ref)):
            cols = slice(t * h, (t + 1) * h)
            xv = xt_ref[:, cols]
            r = r_ref[block, :]
            for k in range(kb):
                wt_ref[k * q : (k + 1) * q, cols] = xv * r[k : k + 1, :]
            wt_ref[kb * q :, cols] = r

    for half in range(2):

        @pl.when(j == half)
        def _():
            cols = slice(half * HALF, (half + 1) * HALF)
            rows = jnp.concatenate([xa_ref[:, cols], xb_ref[:, cols]], axis=0)
            y = jnp.dot(wt_ref[...], rows, preferred_element_type=f32)
            o_ref[...] = y[: kb * q].reshape(kb, q, HALF)
            fm_ref[...] = y[kb * q :]


def sec(ra, rb, xt, xa, xb, kb=16):
    k, _ = ra.shape
    q, n = xt.shape
    whole = pl.BlockSpec(memory_space=pltpu.VMEM)
    return pl.pallas_call(
        functools.partial(sec_kernel, kb=kb),
        grid=(k // kb, 2),
        in_specs=[whole] * 5,
        out_specs=[
            pl.BlockSpec((kb, q, HALF), lambda i, j: (i, 0, j)),
            pl.BlockSpec((kb, HALF), lambda i, j: (i, j)),
            pl.BlockSpec((1, k), lambda i, j: (0, 0)),
        ],
        out_shape=[
            jax.ShapeDtypeStruct((k, q, D), f32),
            jax.ShapeDtypeStruct((k, D), f32),
            jax.ShapeDtypeStruct((1, k), f32),
        ],
        scratch_shapes=[pltpu.VMEM((kb * q + kb, n), bf16)],
        compiler_params=pltpu.CompilerParams(vmem_limit_bytes=VMEM),
        cost_estimate=pl.CostEstimate(
            flops=2 * k * q * D * n, bytes_accessed=4 * k * q * D + 2 * n * D, transcendentals=0
        ),
        name="sec",
    )(ra, rb, xt, xa, xb)


def swap(x, axis):
    return lax.ppermute(x, axis, [(0, 1), (1, 0)])


def after(x, y):
    return lax.optimization_barrier((x, y))[0]


def log_sum(values):
    peak = jnp.max(values, axis=0)
    return peak + jnp.log(jnp.sum(jnp.exp(values - peak[None]), axis=0))


def layer(points, centres, whitening, log_prior):
    pos = (lax.axis_index("xl") * 2 + lax.axis_index("c")).astype(jnp.int32).reshape(1)
    chips = lax.psum(1, CHIPS)
    groups = lax.psum(1, COMP)
    whitening = pltpu.with_memory_space_constraint(whitening, pltpu.HBM)

    m = points.size // 128
    pieces = jnp.broadcast_to(points.reshape(1, m, 128), (chips, m, 128))
    xa = lax.all_to_all(pieces, CHIPS, 0, 0, tiled=True)
    xa = to_rows(xa)
    off, ld = prep(pos, whitening, centres)
    h = xa.shape[0]
    cut = 2 * h // 3
    send1, w = dist(whitening, off, ld, xa, 0, cut, first=True)
    xb = swap(after(xa, send1), "c")
    send2 = dist(w, off, ld, xa, cut, h - cut)
    got1 = swap(after(send1, send2), "c")
    got2 = swap(send2, "c")
    chip1 = dist(w, off, ld, xb, 0, cut) + got1
    far1 = swap(chip1, "xl")
    keep2 = dist(w, off, ld, xb, cut, h - cut)
    chip2 = keep2 + got2
    far2 = swap(chip2, "xl")
    total_b = jnp.concatenate([chip1 + far1, chip2 + far2], axis=1)
    total_a = swap(total_b, "c")
    xt = band(pos, xa, xb)

    logits_a = BETA * (log_prior[:, None] - total_a / D)
    logits_b = BETA * (log_prior[:, None] - total_b / D)
    lse = jnp.concatenate([log_sum(logits_a), log_sum(logits_b)])
    lanes = jnp.broadcast_to(lse.reshape(1, 1, 2 * h), (groups, 1, 2 * h))
    others = lax.all_to_all(lanes, COMP, 0, 0, tiled=True)
    norm = log_sum(others.reshape(groups, 2 * h))
    ra = jnp.exp(logits_a - norm[None, :h]).astype(bf16)
    rb = jnp.exp(logits_b - norm[None, h:]).astype(bf16)
    second, first, counts = sec(ra, rb, xt, xa, xb)
    return counts.reshape(-1), first, second


def solution(mesh):
    fine = Mesh(mesh.devices.reshape(2, 2, 2, 4, 4), ALL)
    band_axes = ("xl", "c")
    in_specs = (P(ALL, None), P(COMP, None), P(COMP, band_axes, None), P(COMP))
    out_specs = (P(COMP), P(COMP, None), P(COMP, band_axes, None))
    return jax.shard_map(layer, mesh=fine, in_specs=in_specs, out_specs=out_specs, check_vma=False)
```
